256 devices in a mesh: seq: 64 (over z, x, core), head: 4 (over y).
Axes of the slice: x: 4, y: 4, z: 8, core: 2. Of those that a mesh axis runs over, the one named last changes fastest.
Arguments:
- queries: bfloat16 [65536, 2048], P('seq', 'head'), may hold values from -14 to 14, as said below
- key_vectors: bfloat16 [65536, 2048], P('seq', 'head'), may hold values from -6 to 6
- value_vectors: bfloat16 [65536, 2048], P('seq', 'head'), may hold values from -20 to 20, as said below
- cotangent: bfloat16 [65536, 2048], P('seq', 'head'), may hold values from -6 to 6
- norm_gain: float32 [2048], P('head'), may hold values from 0.5 to 2
Outputs:
- mixed: bfloat16 [65536, 2048], P('seq', 'head')
- grad_queries: bfloat16 [65536, 2048], P('seq', 'head')
- grad_keys: bfloat16 [65536, 2048], P('seq', 'head')
- grad_values: bfloat16 [65536, 2048], P('seq', 'head')
The draws below stay inside these ranges and needn't reach their ends.
Inputs may be any that keep to these rules, and one draw needn't show every extreme that they name: `queries`: real values. `value_vectors`: real values.
All inputs are finite; a program needn't handle non-finite values.
Results may differ from the reference program's by a relative error of at most 0.013.
Values may be sent and summed in bfloat16 or wider, within the bound.
No kernel may reach another device: no remote copies, remote signals or barrier semaphores. Data moves between devices by JAX's collectives and lax.ppermute only.
A program may use at most 128 MiB of HBM per device.

```python
import math
import jax
import jax.numpy as jnp
from jax import lax

HEADS = 16
HEAD_DIM = 128
TOK_DEV = 1024
WIDTH = 2048
TOKENS = 65536
N_SEQ = 64


def draw_queries(key, part):
    key_scale, key_entries = jax.random.split(jax.random.fold_in(key, 11))
    row_scale = jnp.exp(jax.random.uniform(key_scale, (TOKENS, 1), jnp.float32, 0.0, math.log(10.0)))
    entries = jnp.clip(jax.random.normal(key_entries, (TOKENS, WIDTH), jnp.float32), -4.0, 4.0)
    return (entries * row_scale / 3.0).astype(jnp.bfloat16)


def draw_value_vectors(key, part):
    key_scale, key_entries = jax.random.split(jax.random.fold_in(key, 23))
    column = jnp.arange(WIDTH).astype(jnp.float32)
    rising = jnp.exp(math.log(3.0) * column / (WIDTH - 1))
    column_scale = jnp.exp(jax.random.uniform(key_scale, (1, WIDTH), jnp.float32, 0.0, math.log(10.0))) * rising[None, :]
    entries = jnp.clip(jax.random.normal(key_entries, (TOKENS, WIDTH), jnp.float32), -4.0, 4.0)
    return (entries * column_scale / 6.0).astype(jnp.bfloat16)


def shard_levels(key, shape, cuts, least, largest):
    gain = 1.0
    for position, parts in cuts:
        draws = jax.random.uniform(jax.random.fold_in(jax.random.fold_in(key, 6), position), (parts,), jnp.float32, least / len(cuts), largest / len(cuts))
        gain = gain * jnp.repeat(jnp.exp(draws), shape[position] // parts).reshape((-1,) + (1,) * (len(shape) - 1 - position))
    return gain


def noise(rng, dims, deviation, most, cuts=(), kind=jnp.bfloat16):
    values = deviation * jax.random.normal(rng, dims, jnp.float32)
    if cuts:
        values = values * shard_levels(rng, dims, cuts, -0.22, 0.18)
    return jnp.clip(values, -most, most).astype(kind)


def setup_inputs(seed: int = 0) -> dict:
    arg_keys = jax.random.split(jax.random.key(seed), 6)
    queries = draw_queries(jax.random.fold_in(arg_keys[5], 71), 0)
    key_vectors = noise(arg_keys[1], (TOKENS, WIDTH), 1.0, 6.0, ((0, 64), (1, 4)))
    value_vectors = draw_value_vectors(jax.random.fold_in(arg_keys[5], 71), 0)
    cotangent = noise(arg_keys[3], (TOKENS, WIDTH), 1.0, 6.0, ((0, 64), (1, 4)))
    norm_gain = jnp.clip(jnp.exp(math.log(2.0) - 1.3862944 * jax.random.uniform(arg_keys[4], (WIDTH,), jnp.float32) ** shard_levels(arg_keys[4], (WIDTH,), ((0, 4),), -0.2, 0.2)), 0.5, 2.0)
    return {"queries": queries, "key_vectors": key_vectors, "value_vectors": value_vectors, "cotangent": cotangent, "norm_gain": norm_gain}


epsilon = 1e-06

def reference(queries, key_vectors, value_vectors, cotangent, norm_gain):
    fshape = (N_SEQ, TOK_DEV, HEADS, HEAD_DIM)
    query_blocks = queries.reshape(fshape)
    key_blocks = key_vectors.reshape(fshape)
    value_blocks = value_vectors.reshape(fshape)
    cot_blocks = cotangent.reshape(N_SEQ, TOK_DEV, WIDTH)
    causal = jnp.arange(TOK_DEV)[:, None] >= jnp.arange(TOK_DEV)[None, :]

    def block_state(pair):
        return jnp.einsum('thd,the->hde', pair[0].astype(jnp.float32), pair[1].astype(jnp.float32)).astype(jnp.bfloat16)
    states = lax.map(block_state, (key_blocks, value_blocks))
    running = jnp.cumsum(states.astype(jnp.float32), axis=0)
    prefix = jnp.concatenate([jnp.zeros_like(running[:1]), running[:-1]], axis=0).astype(jnp.bfloat16)

    def make_weights(query, keyrow):
        scores = jnp.einsum('thd,shd->hts', query.astype(jnp.float32), keyrow.astype(jnp.float32))
        return jnp.where(causal[None], scores, 0.0).astype(jnp.bfloat16)

    def forward(items):
        query, keyrow, value, upstream_in, earlier = items
        weights = make_weights(query, keyrow)
        attn = jnp.einsum('hts,shd->thd', weights.astype(jnp.float32), value.astype(jnp.float32))
        attn = attn + jnp.einsum('thd,hde->the', query.astype(jnp.float32), earlier.astype(jnp.float32))
        flat = attn.reshape(TOK_DEV, WIDTH)
        inv = lax.rsqrt(lax.optimization_barrier(jnp.sum(flat * flat, axis=1)) / WIDTH + epsilon)
        mixed = (flat * inv[:, None] * norm_gain).astype(jnp.bfloat16)
        upstream = upstream_in.astype(jnp.float32) * norm_gain
        dots = lax.optimization_barrier(jnp.sum(upstream * flat, axis=1))
        grad_attn = (inv[:, None] * (upstream - flat * (inv * inv * dots / WIDTH)[:, None])).astype(jnp.bfloat16)
        grad_heads = grad_attn.reshape(TOK_DEV, HEADS, HEAD_DIM)
        term = jnp.einsum('thd,the->hde', query.astype(jnp.float32), grad_heads.astype(jnp.float32)).astype(jnp.bfloat16)
        return (mixed, grad_heads, term)
    mixed, grad_heads, terms = lax.map(forward, (query_blocks, key_blocks, value_blocks, cot_blocks, prefix))
    backsum = jnp.cumsum(terms.astype(jnp.float32)[::-1], axis=0)[::-1]
    suffix = jnp.concatenate([backsum[1:], jnp.zeros_like(backsum[:1])], axis=0).astype(jnp.bfloat16)

    def backward(items):
        query, keyrow, value, grad, earlier, later = items
        qf = query.astype(jnp.float32)
        kf = keyrow.astype(jnp.float32)
        vf = value.astype(jnp.float32)
        gf = grad.astype(jnp.float32)
        ef = earlier.astype(jnp.float32)
        lf = later.astype(jnp.float32)
        weights = make_weights(query, keyrow).astype(jnp.float32)
        dscores = jnp.einsum('thd,shd->hts', gf, vf)
        dweights = jnp.where(causal[None], dscores, 0.0).astype(jnp.bfloat16).astype(jnp.float32)
        grad_q = jnp.einsum('hts,shd->thd', dweights, kf) + jnp.einsum('the,hde->thd', gf, ef)
        grad_k = jnp.einsum('hts,thd->shd', dweights, qf) + jnp.einsum('the,hde->thd', vf, lf)
        grad_v = jnp.einsum('hts,thd->shd', weights, gf) + jnp.einsum('thd,hde->the', kf, lf)
        return (grad_q.reshape(TOK_DEV, WIDTH).astype(jnp.bfloat16), grad_k.reshape(TOK_DEV, WIDTH).astype(jnp.bfloat16), grad_v.reshape(TOK_DEV, WIDTH).astype(jnp.bfloat16))
    grad_q, grad_k, grad_v = lax.map(backward, (query_blocks, key_blocks, value_blocks, grad_heads, prefix, suffix))
    return (mixed.reshape(TOKENS, WIDTH), grad_q.reshape(TOKENS, WIDTH), grad_k.reshape(TOKENS, WIDTH), grad_v.reshape(TOKENS, WIDTH))
```

```python
import jax
import jax.numpy as jnp
from jax import lax
from jax.experimental import pallas as pl
from jax.experimental.pallas import tpu as pltpu
from jax.sharding import PartitionSpec as P

HEAD_DIM = 128
WIDTH = 2048
epsilon = 1e-06
ROWS = 256

f32 = jnp.float32
bf16 = jnp.bfloat16


def nn(a, b):
    return lax.dot_general(a, b, (((1,), (0,)), ((), ())), preferred_element_type=f32)


def nt(a, b):
    return lax.dot_general(a, b, (((1,), (1,)), ((), ())), preferred_element_type=f32)


def tn(a, b):
    return lax.dot_general(a, b, (((0,), (0,)), ((), ())), preferred_element_type=f32)


def params(mib=24):
    return pltpu.CompilerParams(vmem_limit_bytes=mib << 20)


def cost(flops, nbytes):
    return pl.CostEstimate(flops=flops, bytes_accessed=nbytes, transcendentals=0)


def outer_kernel(a_ref, b_ref, s_ref, acc_ref):
    step = pl.program_id(0)

    @pl.when(step == 0)
    def _():
        acc_ref[...] = jnp.zeros_like(acc_ref)

    pairs = acc_ref.shape[0]
    for p in range(pairs):
        cols = slice(p * 256, p * 256 + 256)
        acc_ref[p] += tn(a_ref[:, cols], b_ref[:, cols])

    @pl.when(step == pl.num_programs(0) - 1)
    def _():
        for p in range(pairs):
            s_ref[2 * p] = acc_ref[p, :128, :128].astype(bf16)
            s_ref[2 * p + 1] = acc_ref[p, 128:, 128:].astype(bf16)


def block_state(a, b):
    t, c = a.shape
    heads = c // HEAD_DIM
    spec = pl.BlockSpec((ROWS, c), lambda i: (i, 0))
    return pl.pallas_call(
        outer_kernel,
        grid=(t // ROWS,),
        in_specs=[spec, spec],
        out_specs=pl.BlockSpec((heads, 128, 128), lambda i: (0, 0, 0)),
        out_shape=jax.ShapeDtypeStruct((heads, 128, 128), bf16),
        scratch_shapes=[pltpu.VMEM((heads // 2, 256, 256), f32)],
        compiler_params=params(8),
        cost_estimate=cost(2 * t * c * 256, 2 * t * c * 2),
        name="block_state",
    )(a, b)


def masked(x, r, c0, upper=False):
    row = lax.broadcasted_iota(jnp.int32, x.shape, 0) + r
    col = lax.broadcasted_iota(jnp.int32, x.shape, 1) + c0
    keep = (row <= col) if upper else (row >= col)
    return jnp.where(keep, x, 0.0).astype(bf16)


def local_kernel(q_ref, k_ref, v_ref, o_ref):
    t, c = q_ref.shape
    for h in range(c // HEAD_DIM):
        cols = slice(h * HEAD_DIM, (h + 1) * HEAD_DIM)
        for r in range(0, t, ROWS):
            q = q_ref[r : r + ROWS, cols]
            w = masked(nt(q, k_ref[r : r + ROWS, cols]), 0, 0)
            o = nn(w, v_ref[r : r + ROWS, cols])
            if r:
                w = nt(q, k_ref[:r, cols]).astype(bf16)
                o = o + nn(w, v_ref[:r, cols])
            o_ref[r : r + ROWS, cols] = o


def local_attn(q, k, v, part, parts):
    t, c = q.shape
    w = c // parts
    spec = pl.BlockSpec((t, w), lambda i: (0, part))
    return pl.pallas_call(
        local_kernel,
        grid=(1,),
        in_specs=[spec] * 3,
        out_specs=pl.BlockSpec((t, w), lambda i: (0, 0)),
        out_shape=jax.ShapeDtypeStruct((t, w), f32),
        compiler_params=params(24),
        cost_estimate=cost(2 * 2 * t * t * w * 5 // 8, t * w * 10),
        name="local_attn",
    )(q, k, v)


def row_sums(x):
    acc = x[:, :128]
    for g in range(1, x.shape[1] // 128):
        acc = acc + x[:, g * 128 : (g + 1) * 128]
    return jnp.sum(acc.T, axis=0, keepdims=True)


def column(row):
    return jnp.broadcast_to(row, (128, row.shape[1])).T


def attn_kernel(*refs):
    n = len(refs) - 6
    o_refs = refs[:n]
    q_ref, p_ref, y_ref, g_ref, attn_ref, stat_ref = refs[n:]
    w = o_refs[0].shape[1]
    for h in range(q_ref.shape[1] // HEAD_DIM):
        cols = slice(h * HEAD_DIM, (h + 1) * HEAD_DIM)
        at = h * HEAD_DIM
        own = o_refs[at // w][:, at % w : at % w + HEAD_DIM]
        attn_ref[:, cols] = own + nn(q_ref[:, cols], p_ref[h])
    attn = attn_ref[...]
    up = y_ref[...].astype(f32) * g_ref[...]
    stat_ref[0:1, :] = row_sums(attn * attn)
    stat_ref[1:2, :] = row_sums(up * attn)


def attn_stats(locals_, q, prefix, y, gain):
    t, c = q.shape
    w = locals_[0].shape[1]
    wide = pl.BlockSpec((ROWS, c), lambda i: (i, 0))
    return pl.pallas_call(
        attn_kernel,
        grid=(t // ROWS,),
        in_specs=[pl.BlockSpec((ROWS, w), lambda i: (i, 0))] * len(locals_)
        + [
            wide,
            pl.BlockSpec(prefix.shape, lambda i: (0, 0, 0)),
            wide,
            pl.BlockSpec((1, c), lambda i: (0, 0)),
        ],
        out_specs=(wide, pl.BlockSpec((2, ROWS), lambda i: (0, i))),
        out_shape=(jax.ShapeDtypeStruct((t, c), f32), jax.ShapeDtypeStruct((2, t), f32)),
        compiler_params=params(12),
        cost_estimate=cost(2 * t * c * 128, t * c * 12),
        name="attn_stats",
    )(*locals_, q, prefix, y, gain)


def grad_kernel(attn_ref, y_ref, q_ref, stat_ref, g_ref, mixed_ref, d_ref, term_ref, acc_ref):
    step = pl.program_id(0)

    @pl.when(step == 0)
    def _():
        acc_ref[...] = jnp.zeros_like(acc_ref)

    inv_row = lax.rsqrt(stat_ref[0:1, :] / WIDTH + epsilon)
    scale_row = inv_row * inv_row * stat_ref[1:2, :] / WIDTH
    inv = column(inv_row)
    scale = column(scale_row)
    for h in range(q_ref.shape[1] // HEAD_DIM):
        cols = slice(h * HEAD_DIM, (h + 1) * HEAD_DIM)
        attn = attn_ref[:, cols]
        gain = g_ref[:, cols]
        mixed_ref[:, cols] = (attn * inv * gain).astype(bf16)
        up = y_ref[:, cols].astype(f32) * gain
        d_ref[:, cols] = (inv * (up - attn * scale)).astype(bf16)
    pairs = acc_ref.shape[0]
    for p in range(pairs):
        cols = slice(p * 256, p * 256 + 256)
        acc_ref[p] += tn(q_ref[:, cols], d_ref[:, cols])

    @pl.when(step == pl.num_programs(0) - 1)
    def _():
        for p in range(pairs):
            term_ref[2 * p] = acc_ref[p, :128, :128].astype(bf16)
            term_ref[2 * p + 1] = acc_ref[p, 128:, 128:].astype(bf16)


def grads_of_norm(attn, y, q, stats, gain):
    t, c = q.shape
    heads = c // HEAD_DIM
    wide = pl.BlockSpec((ROWS, c), lambda i: (i, 0))
    return pl.pallas_call(
        grad_kernel,
        grid=(t // ROWS,),
        in_specs=[
            wide,
            wide,
            wide,
            pl.BlockSpec((2, ROWS), lambda i: (0, i)),
            pl.BlockSpec((1, c), lambda i: (0, 0)),
        ],
        out_specs=(wide, wide, pl.BlockSpec((heads, 128, 128), lambda i: (0, 0, 0))),
        out_shape=(
            jax.ShapeDtypeStruct((t, c), bf16),
            jax.ShapeDtypeStruct((t, c), bf16),
            jax.ShapeDtypeStruct((heads, 128, 128), bf16),
        ),
        scratch_shapes=[pltpu.VMEM((heads // 2, 256, 256), f32)],
        compiler_params=params(12),
        cost_estimate=cost(2 * t * c * 256, t * c * 12),
        name="grads_of_norm",
    )(attn, y, q, stats, gain)


def back_kernel(q_ref, k_ref, v_ref, d_ref, p_ref, dq_ref, dk_ref, dv_ref):
    t, c = q_ref.shape
    for h in range(c // HEAD_DIM):
        cols = slice(h * HEAD_DIM, (h + 1) * HEAD_DIM)
        for r in range(0, t, ROWS):
            here = slice(r, r + ROWS)
            q, k, v, d = q_ref[here, cols], k_ref[here, cols], v_ref[here, cols], d_ref[here, cols]
            dq = nt(d, p_ref[h]) + nn(masked(nt(d, v), 0, 0), k)
            if r:
                dq = dq + nn(nt(d, v_ref[:r, cols]).astype(bf16), k_ref[:r, cols])
            dq_ref[here, cols] = dq.astype(bf16)
            dk = nn(masked(nt(v, d), 0, 0, True), q)
            dv = nn(masked(nt(k, q), 0, 0, True), d)
            e = r + ROWS
            if e < t:
                dk = dk + nn(nt(v, d_ref[e:, cols]).astype(bf16), q_ref[e:, cols])
                dv = dv + nn(nt(k, q_ref[e:, cols]).astype(bf16), d_ref[e:, cols])
            dk_ref[here, cols] = dk
            dv_ref[here, cols] = dv


def local_back(q, k, v, d, prefix, part, parts):
    t, c = q.shape
    w = c // parts
    spec = pl.BlockSpec((t, w), lambda i: (0, part))
    out = pl.BlockSpec((t, w), lambda i: (0, 0))
    return pl.pallas_call(
        back_kernel,
        grid=(1,),
        in_specs=[spec] * 4 + [pl.BlockSpec((w // 128, 128, 128), lambda i: (part, 0, 0))],
        out_specs=(out,) * 3,
        out_shape=(
            jax.ShapeDtypeStruct((t, w), bf16),
            jax.ShapeDtypeStruct((t, w), f32),
            jax.ShapeDtypeStruct((t, w), f32),
        ),
        compiler_params=params(24),
        cost_estimate=cost(6 * 2 * t * t * w * 5 // 8, t * w * 18),
        name="local_back",
    )(q, k, v, d, prefix)


def final_kernel(*refs):
    n = (len(refs) - 5) // 2
    dk_refs, dv_refs = refs[:n], refs[n : 2 * n]
    k_ref, v_ref, s_ref, ok_ref, ov_ref = refs[2 * n :]
    w = dk_refs[0].shape[1]
    for h in range(k_ref.shape[1] // HEAD_DIM):
        cols = slice(h * HEAD_DIM, (h + 1) * HEAD_DIM)
        at = h * HEAD_DIM
        part = slice(at % w, at % w + HEAD_DIM)
        ok_ref[:, cols] = (dk_refs[at // w][:, part] + nt(v_ref[:, cols], s_ref[h])).astype(bf16)
        ov_ref[:, cols] = (dv_refs[at // w][:, part] + nn(k_ref[:, cols], s_ref[h])).astype(bf16)


def finish(dks, dvs, k, v, suffix):
    t, c = k.shape
    w = dks[0].shape[1]
    wide = pl.BlockSpec((ROWS, c), lambda i: (i, 0))
    return pl.pallas_call(
        final_kernel,
        grid=(t // ROWS,),
        in_specs=[pl.BlockSpec((ROWS, w), lambda i: (i, 0))] * (2 * len(dks))
        + [wide, wide, pl.BlockSpec(suffix.shape, lambda i: (0, 0, 0))],
        out_specs=(wide, wide),
        out_shape=(jax.ShapeDtypeStruct((t, c), bf16),) * 2,
        compiler_params=params(16),
        cost_estimate=cost(4 * t * c * 128, t * c * 16),
        name="finish",
    )(*dks, *dvs, k, v, suffix)


NZ, NX = 8, 4


def step_pairs(reverse, dz=0, dx=0, swap=False):
    pairs = []
    for i in range(NZ * NX * 2):
        z, x, c = i // 8, (i // 2) % 4, i % 2
        z2 = z + dz
        if not 0 <= z2 < NZ:
            continue
        j = (z2 * NX + (x + dx) % NX) * 2 + (1 - c if swap else c)
        pairs.append((63 - i, 63 - j) if reverse else (i, j))
    return pairs


def exclusive_sum(own, reverse):
    def send(a, **step):
        return lax.ppermute(a, "seq", step_pairs(reverse, **step))

    index = lax.axis_index("seq")
    index = 63 - index if reverse else index
    x, c = (index // 2) % 4, index % 2
    first = c == 0
    n = own.shape[0] // 2
    mine = jnp.where(first, own[:n], own[n:])
    other = jnp.where(first, own[n:], own[:n])
    got = send(other, swap=True)
    chip = (mine.astype(f32) + got.astype(f32)).astype(bf16)
    row = chip.astype(f32)
    before = jnp.zeros_like(row)
    for k in (2, 1, 3):
        r = send(chip, dx=k).astype(f32)
        row = row + r
        before = before + jnp.where(x >= k, r, 0.0)
    plane = row.astype(bf16)
    near = send(plane, dz=2).astype(f32) + send(plane, dz=1).astype(f32)
    three = (row + near).astype(bf16)
    far = send(three, dz=3).astype(f32) + send(three, dz=6).astype(f32)
    e0 = before + near + far
    e1 = e0 + jnp.where(first, mine, got).astype(f32)
    e0, e1 = e0.astype(bf16), e1.astype(bf16)
    keep = jnp.where(first, e0, e1)
    back = send(jnp.where(first, e1, e0), swap=True)
    return jnp.where(first, jnp.concatenate([keep, back]), jnp.concatenate([back, keep]))


def head_sum(a):
    r = [lax.ppermute(a, "head", [(i, (i + k) % 4) for i in range(4)]) for k in (2, 1, 3)]
    return a + r[0] + r[1] + r[2]


FWD, BWD = 2, 4


def shards(q, k, v, y, gain):
    gain = gain[None, :]
    prefix = exclusive_sum(block_state(k, v), False)
    locals_ = [local_attn(q, k, v, i, FWD) for i in range(FWD)]
    attn, stats = attn_stats(locals_, q, prefix, y, gain)
    stats = head_sum(stats)
    mixed, d, term = grads_of_norm(attn, y, q, stats, gain)
    suffix = exclusive_sum(term, True)
    parts = [local_back(q, k, v, d, prefix, i, BWD) for i in range(BWD)]
    dk, dv = finish([p[1] for p in parts], [p[2] for p in parts], k, v, suffix)
    return mixed, jnp.concatenate([p[0] for p in parts], axis=1), dk, dv


def solution(mesh):
    wide = P("seq", "head")
    return jax.shard_map(
        shards,
        mesh=mesh,
        in_specs=(wide, wide, wide, wide, P("head")),
        out_specs=(wide, wide, wide, wide),
        check_vma=False,
    )
```

```python
import jax
import jax.numpy as jnp
from jax import lax
from jax.experimental import pallas as pl
from jax.experimental.pallas import tpu as pltpu
from jax.sharding import PartitionSpec as P


HEAD_DIM = 128
WIDTH = 2048
epsilon = 1e-06
ROWS = 256

f32 = jnp.float32
bf16 = jnp.bfloat16


def nn(a, b):
    return lax.dot_general(a, b, (((1,), (0,)), ((), ())), preferred_element_type=f32)


def nt(a, b):
    return lax.dot_general(a, b, (((1,), (1,)), ((), ())), preferred_element_type=f32)


def tn(a, b):
    return lax.dot_general(a, b, (((0,), (0,)), ((), ())), preferred_element_type=f32)


def params(mib=24):
    return pltpu.CompilerParams(vmem_limit_bytes=mib << 20)


def cost(flops, nbytes):
    return pl.CostEstimate(flops=flops, bytes_accessed=nbytes, transcendentals=0)


def outer_kernel(a_ref, b_ref, s_ref, acc_ref):
    step = pl.program_id(0)

    @pl.when(step == 0)
    def _():
        acc_ref[...] = jnp.zeros_like(acc_ref)

    pairs = acc_ref.shape[0]
    for p in range(pairs):
        cols = slice(p * 256, p * 256 + 256)
        acc_ref[p] += tn(a_ref[:, cols], b_ref[:, cols])

    @pl.when(step == pl.num_programs(0) - 1)
    def _():
        for p in range(pairs):
            s_ref[2 * p] = acc_ref[p, :128, :128].astype(bf16)
            s_ref[2 * p + 1] = acc_ref[p, 128:, 128:].astype(bf16)


def block_state(a, b):
    t, c = a.shape
    heads = c // HEAD_DIM
    spec = pl.BlockSpec((ROWS, c), lambda i: (i, 0))
    return pl.pallas_call(
        outer_kernel,
        grid=(t // ROWS,),
        in_specs=[spec, spec],
        out_specs=pl.BlockSpec((heads, 128, 128), lambda i: (0, 0, 0)),
        out_shape=jax.ShapeDtypeStruct((heads, 128, 128), bf16),
        scratch_shapes=[pltpu.VMEM((heads // 2, 256, 256), f32)],
        compiler_params=params(8),
        cost_estimate=cost(2 * t * c * 256, 2 * t * c * 2),
        name="block_state",
    )(a, b)


def masked(x, r, c0, upper=False):
    row = lax.broadcasted_iota(jnp.int32, x.shape, 0) + r
    col = lax.broadcasted_iota(jnp.int32, x.shape, 1) + c0
    keep = (row <= col) if upper else (row >= col)
    return jnp.where(keep, x, 0.0).astype(bf16)


def local_kernel(q_ref, k_ref, v_ref, o_ref):
    t, c = q_ref.shape
    for h in range(c // HEAD_DIM):
        cols = slice(h * HEAD_DIM, (h + 1) * HEAD_DIM)
        for r in range(0, t, ROWS):
            q = q_ref[r : r + ROWS, cols]
            w = masked(nt(q, k_ref[r : r + ROWS, cols]), 0, 0)
            o = nn(w, v_ref[r : r + ROWS, cols])
            if r:
                w = nt(q, k_ref[:r, cols]).astype(bf16)
                o = o + nn(w, v_ref[:r, cols])
            o_ref[r : r + ROWS, cols] = o


def local_attn(q, k, v, part, parts):
    t, c = q.shape
    w = c // parts
    spec = pl.BlockSpec((t, w), lambda i: (0, part))
    return pl.pallas_call(
        local_kernel,
        grid=(1,),
        in_specs=[spec] * 3,
        out_specs=pl.BlockSpec((t, w), lambda i: (0, 0)),
        out_shape=jax.ShapeDtypeStruct((t, w), f32),
        compiler_params=params(24),
        cost_estimate=cost(2 * 2 * t * t * w * 5 // 8, t * w * 10),
        name="local_attn",
    )(q, k, v)


def row_sums(x):
    acc = x[:, :128]
    for g in range(1, x.shape[1] // 128):
        acc = acc + x[:, g * 128 : (g + 1) * 128]
    return jnp.sum(acc.T, axis=0, keepdims=True)


def column(row):
    return jnp.broadcast_to(row, (128, row.shape[1])).T


def attn_kernel(*refs):
    n = len(refs) - 6
    o_refs = refs[:n]
    q_ref, p_ref, y_ref, g_ref, attn_ref, stat_ref = refs[n:]
    w = o_refs[0].shape[1]
    for h in range(q_ref.shape[1] // HEAD_DIM):
        cols = slice(h * HEAD_DIM, (h + 1) * HEAD_DIM)
        at = h * HEAD_DIM
        own = o_refs[at // w][:, at % w : at % w + HEAD_DIM]
        attn_ref[:, cols] = own + nn(q_ref[:, cols], p_ref[h])
    attn = attn_ref[...]
    up = y_ref[...].astype(f32) * g_ref[...]
    stat_ref[0:1, :] = row_sums(attn * attn)
    stat_ref[1:2, :] = row_sums(up * attn)


def attn_stats(locals_, q, prefix, y, gain):
    t, c = q.shape
    w = locals_[0].shape[1]
    wide = pl.BlockSpec((ROWS, c), lambda i: (i, 0))
    return pl.pallas_call(
        attn_kernel,
        grid=(t // ROWS,),
        in_specs=[pl.BlockSpec((ROWS, w), lambda i: (i, 0))] * len(locals_)
        + [
            wide,
            pl.BlockSpec(prefix.shape, lambda i: (0, 0, 0)),
            wide,
            pl.BlockSpec((1, c), lambda i: (0, 0)),
        ],
        out_specs=(wide, pl.BlockSpec((2, ROWS), lambda i: (0, i))),
        out_shape=(jax.ShapeDtypeStruct((t, c), f32), jax.ShapeDtypeStruct((2, t), f32)),
        compiler_params=params(12),
        cost_estimate=cost(2 * t * c * 128, t * c * 12),
        name="attn_stats",
    )(*locals_, q, prefix, y, gain)


def grad_kernel(attn_ref, y_ref, q_ref, s0, s1, s2, s3, g_ref, mixed_ref, d_ref, term_ref, acc_ref):
    step = pl.program_id(0)

    @pl.when(step == 0)
    def _():
        acc_ref[...] = jnp.zeros_like(acc_ref)

    stat = (s0[...] + s1[...]) + (s2[...] + s3[...])
    inv_row = lax.rsqrt(stat[0:1, :] / WIDTH + epsilon)
    scale_row = inv_row * inv_row * stat[1:2, :] / WIDTH
    inv = column(inv_row)
    scale = column(scale_row)
    for h in range(q_ref.shape[1] // HEAD_DIM):
        cols = slice(h * HEAD_DIM, (h + 1) * HEAD_DIM)
        attn = attn_ref[:, cols]
        gain = g_ref[:, cols]
        mixed_ref[:, cols] = (attn * inv * gain).astype(bf16)
        up = y_ref[:, cols].astype(f32) * gain
        d_ref[:, cols] = (inv * (up - attn * scale)).astype(bf16)
    pairs = acc_ref.shape[0]
    for p in range(pairs):
        cols = slice(p * 256, p * 256 + 256)
        acc_ref[p] += tn(q_ref[:, cols], d_ref[:, cols])

    @pl.when(step == pl.num_programs(0) - 1)
    def _():
        for p in range(pairs):
            term_ref[2 * p] = acc_ref[p, :128, :128].astype(bf16)
            term_ref[2 * p + 1] = acc_ref[p, 128:, 128:].astype(bf16)


def grads_of_norm(attn, y, q, stats, gain):
    t, c = q.shape
    heads = c // HEAD_DIM
    wide = pl.BlockSpec((ROWS, c), lambda i: (i, 0))
    return pl.pallas_call(
        grad_kernel,
        grid=(t // ROWS,),
        in_specs=[
            wide,
            wide,
            wide,
            *[pl.BlockSpec((2, ROWS), lambda i: (0, i))] * 4,
            pl.BlockSpec((1, c), lambda i: (0, 0)),
        ],
        out_specs=(wide, wide, pl.BlockSpec((heads, 128, 128), lambda i: (0, 0, 0))),
        out_shape=(
            jax.ShapeDtypeStruct((t, c), bf16),
            jax.ShapeDtypeStruct((t, c), bf16),
            jax.ShapeDtypeStruct((heads, 128, 128), bf16),
        ),
        scratch_shapes=[pltpu.VMEM((heads // 2, 256, 256), f32)],
        compiler_params=params(12),
        cost_estimate=cost(2 * t * c * 256, t * c * 12),
        name="grads_of_norm",
    )(attn, y, q, *stats, gain)


def back_kernel(q_ref, k_ref, v_ref, d_ref, p_ref, *refs):
    dq_ref, dk_ref, dv_ref = refs[-3:]
    t, c = q_ref.shape
    for h in range(c // HEAD_DIM):
        cols = slice(h * HEAD_DIM, (h + 1) * HEAD_DIM)
        for r in range(0, t, ROWS):
            here = slice(r, r + ROWS)
            q, k, v, d = q_ref[here, cols], k_ref[here, cols], v_ref[here, cols], d_ref[here, cols]
            dq = nt(d, p_ref[h]) + nn(masked(nt(d, v), 0, 0), k)
            if r:
                dq = dq + nn(nt(d, v_ref[:r, cols]).astype(bf16), k_ref[:r, cols])
            dq_ref[here, cols] = dq.astype(bf16)
            dk = nn(masked(nt(v, d), 0, 0, True), q)
            dv = nn(masked(nt(k, q), 0, 0, True), d)
            e = r + ROWS
            if e < t:
                dk = dk + nn(nt(v, d_ref[e:, cols]).astype(bf16), q_ref[e:, cols])
                dv = dv + nn(nt(k, q_ref[e:, cols]).astype(bf16), d_ref[e:, cols])
            dk_ref[here, cols] = dk
            dv_ref[here, cols] = dv


def local_back(q, k, v, d, prefix, dq, part, parts):
    t, c = q.shape
    w = c // parts
    spec = pl.BlockSpec((t, w), lambda i: (0, part))
    out = pl.BlockSpec((t, w), lambda i: (0, 0))
    held = [] if dq is None else [dq]
    return pl.pallas_call(
        back_kernel,
        grid=(1,),
        in_specs=[spec] * 4
        + [pl.BlockSpec((w // 128, 128, 128), lambda i: (part, 0, 0))]
        + [pl.BlockSpec(memory_space=pl.ANY)] * len(held),
        out_specs=(spec, out, out),
        input_output_aliases={5: 0} if held else {},
        out_shape=(
            jax.ShapeDtypeStruct((t, c), bf16),
            jax.ShapeDtypeStruct((t, w), f32),
            jax.ShapeDtypeStruct((t, w), f32),
        ),
        compiler_params=params(24),
        cost_estimate=cost(6 * 2 * t * t * w * 5 // 8, t * w * 18),
        name="local_back",
    )(q, k, v, d, prefix, *held)


def final_kernel(*refs):
    n = (len(refs) - 5) // 2
    dk_refs, dv_refs = refs[:n], refs[n : 2 * n]
    k_ref, v_ref, s_ref, ok_ref, ov_ref = refs[2 * n :]
    w = dk_refs[0].shape[1]
    for h in range(k_ref.shape[1] // HEAD_DIM):
        cols = slice(h * HEAD_DIM, (h + 1) * HEAD_DIM)
        at = h * HEAD_DIM
        part = slice(at % w, at % w + HEAD_DIM)
        ok_ref[:, cols] = (dk_refs[at // w][:, part] + nt(v_ref[:, cols], s_ref[h])).astype(bf16)
        ov_ref[:, cols] = (dv_refs[at // w][:, part] + nn(k_ref[:, cols], s_ref[h])).astype(bf16)


def finish(dks, dvs, k, v, suffix):
    t, c = k.shape
    w = dks[0].shape[1]
    wide = pl.BlockSpec((ROWS, c), lambda i: (i, 0))
    return pl.pallas_call(
        final_kernel,
        grid=(t // ROWS,),
        in_specs=[pl.BlockSpec((ROWS, w), lambda i: (i, 0))] * (2 * len(dks))
        + [wide, wide, pl.BlockSpec(suffix.shape, lambda i: (0, 0, 0))],
        out_specs=(wide, wide),
        out_shape=(jax.ShapeDtypeStruct((t, c), bf16),) * 2,
        compiler_params=params(16),
        cost_estimate=cost(4 * t * c * 128, t * c * 16),
        name="finish",
    )(*dks, *dvs, k, v, suffix)


NZ, NX = 8, 4


def step_pairs(reverse, dz=0, dx=0, swap=False):
    pairs = []
    for i in range(NZ * NX * 2):
        z, x, c = i // 8, (i // 2) % 4, i % 2
        j = ((z + dz) % NZ * NX + (x + dx) % NX) * 2 + (1 - c if swap else c)
        pairs.append((63 - i, 63 - j) if reverse else (i, j))
    return pairs


def places(reverse):
    index = lax.axis_index("seq")
    index = 63 - index if reverse else index
    z, x, c = index >> 3, (index >> 1) & 3, index & 1
    low, high = (z + 7) & 7, (z + 1) & 7
    up, down = (z + 3) & 7, (z + 5) & 7
    return (
        c == 0,
        tuple(x >= k for k in (1, 2, 3)),
        z >= 1,
        z == 7,
        (low < up, z < up, high < up),
        (low < down, z < down),
    )


def exclusive_sum(own, reverse, masks):
    def send(a, **step):
        return lax.ppermute(a, "seq", step_pairs(reverse, **step))

    first, west, south, north, up, down = masks
    n = own.shape[0] // 2
    mine = jnp.where(first, own[:n], own[n:])
    other = jnp.where(first, own[n:], own[:n])
    got = send(other, swap=True)
    chip = (mine.astype(f32) + got.astype(f32)).astype(bf16)
    row = chip.astype(f32)
    before = jnp.zeros_like(row)
    for k in (1, 3, 2):
        r = send(chip, dx=k).astype(f32)
        row = row + r
        before = before + jnp.where(west[k - 1], r, 0.0)
    plane = row.astype(bf16)
    below = send(plane, dz=1).astype(f32)
    above = send(plane, dz=-1).astype(f32)
    near = jnp.where(south, below, 0.0) + jnp.where(north, above, 0.0)

    def lacking(flags):
        return sum(jnp.where(m, p, 0.0) for m, p in zip(flags, (below, row, above))).astype(bf16)

    far = send(lacking(up), dz=3).astype(f32)
    far = far + send(lacking(down), dz=-3).astype(f32)
    e0 = before + near + far
    e1 = e0 + jnp.where(first, mine, got).astype(f32)
    e0, e1 = e0.astype(bf16), e1.astype(bf16)
    keep = jnp.where(first, e0, e1)
    back = send(jnp.where(first, e1, e0), swap=True)
    return jnp.where(first, jnp.concatenate([keep, back]), jnp.concatenate([back, keep]))


def head_parts(a):
    return [a] + [
        lax.ppermute(a, "head", [(i, (i + k) % 4) for i in range(4)]) for k in (1, 3, 2)
    ]


PARTS = 4


def shards(q, k, v, y, gain):
    gain = gain[None, :]
    first, last = places(False), places(True)
    first, last, k, v = lax.optimization_barrier((first, last, k, v))
    in_hbm = [pltpu.with_memory_space_constraint(a, pltpu.HBM) for a in (k, v)]
    prefix = exclusive_sum(block_state(*in_hbm), False, first)
    locals_ = []
    for i in range(PARTS):
        locals_.append(local_attn(q, k, v, i, PARTS))
    attn, stats = attn_stats(locals_, q, prefix, y, gain)
    mixed, d, term = grads_of_norm(attn, y, q, head_parts(stats), gain)
    suffix = exclusive_sum(term, True, last)
    dq, dks, dvs = None, [], []
    for i in range(PARTS):
        dq, dk, dv = local_back(q, k, v, d, prefix, dq, i, PARTS)
        dks.append(dk)
        dvs.append(dv)
    dk, dv = finish(dks, dvs, k, v, suffix)
    return mixed, dq, dk, dv


def solution(mesh):
    wide = P("seq", "head")
    return jax.shard_map(
        shards,
        mesh=mesh,
        in_specs=(wide, wide, wide, wide, P("head")),
        out_specs=(wide, wide, wide, wide),
        check_vma=False,
    )
```

```python
import functools

import jax
import jax.numpy as jnp
from jax import lax
from jax.experimental import pallas as pl
from jax.experimental.pallas import tpu as pltpu
from jax.sharding import PartitionSpec as P


HEAD_DIM = 128
WIDTH = 2048
epsilon = 1e-06
ROWS = 256

f32 = jnp.float32
bf16 = jnp.bfloat16


def nn(a, b):
    return lax.dot_general(a, b, (((1,), (0,)), ((), ())), preferred_element_type=f32)


def nt(a, b):
    return lax.dot_general(a, b, (((1,), (1,)), ((), ())), preferred_element_type=f32)


def tn(a, b):
    return lax.dot_general(a, b, (((0,), (0,)), ((), ())), preferred_element_type=f32)


def params(mib=24):
    return pltpu.CompilerParams(vmem_limit_bytes=mib << 20)


def cost(flops, nbytes):
    return pl.CostEstimate(flops=flops, bytes_accessed=nbytes, transcendentals=0)


VMEM = pl.BlockSpec(memory_space=pltpu.VMEM)
ANY = pl.BlockSpec(memory_space=pl.ANY)


def chunk(i):
    return slice(i * ROWS, (i + 1) * ROWS)


def outer_kernel(a_hbm, b_hbm, s_ref, a_ref, b_ref, sems):
    t, c = a_ref.shape
    n = t // ROWS
    copies = []
    for i in range(n):
        for hbm, ref in ((a_hbm, a_ref), (b_hbm, b_ref)):
            rows = pl.ds(i * ROWS, ROWS)
            copy = pltpu.make_async_copy(hbm.at[rows], ref.at[rows], sems.at[len(copies)])
            copy.start()
            copies.append(copy)
    total = [None] * (c // 256)
    for i in range(n):
        copies[2 * i].wait()
        copies[2 * i + 1].wait()
        for p in range(c // 256):
            cols = slice(p * 256, p * 256 + 256)
            x = tn(a_ref[chunk(i), cols], b_ref[chunk(i), cols])
            total[p] = x if i == 0 else total[p] + x
    for p in range(c // 256):
        s_ref[2 * p] = total[p][:128, :128].astype(bf16)
        s_ref[2 * p + 1] = total[p][128:, 128:].astype(bf16)


def block_state(a, b):
    t, c = a.shape
    heads = c // HEAD_DIM
    return pl.pallas_call(
        outer_kernel,
        in_specs=[ANY, ANY],
        out_specs=VMEM,
        out_shape=jax.ShapeDtypeStruct((heads, 128, 128), bf16),
        scratch_shapes=[
            pltpu.VMEM((t, c), bf16),
            pltpu.VMEM((t, c), bf16),
            pltpu.SemaphoreType.DMA((2 * t // ROWS,)),
        ],
        compiler_params=params(8),
        cost_estimate=cost(2 * t * c * 256, 2 * t * c * 2),
        name="block_state",
    )(a, b)


def masked(x, upper=False):
    row = lax.broadcasted_iota(jnp.int32, x.shape, 0)
    col = lax.broadcasted_iota(jnp.int32, x.shape, 1)
    return jnp.where((row <= col) if upper else (row >= col), x, 0.0).astype(bf16)


def local_kernel(head, q_ref, k_ref, v_ref, o_ref):
    t = q_ref.shape[0]
    cols = slice(head * HEAD_DIM, (head + 1) * HEAD_DIM)
    for r in range(0, t, ROWS):
        q = q_ref[r : r + ROWS, cols]
        w = masked(nt(q, k_ref[r : r + ROWS, cols]))
        o = nn(w, v_ref[r : r + ROWS, cols])
        if r:
            w = nt(q, k_ref[:r, cols]).astype(bf16)
            o = o + nn(w, v_ref[:r, cols])
        o_ref[r : r + ROWS, :] = o


def local_attn(q, k, v, head):
    t = q.shape[0]
    return pl.pallas_call(
        functools.partial(local_kernel, head),
        in_specs=[VMEM] * 3,
        out_specs=VMEM,
        out_shape=jax.ShapeDtypeStruct((t, HEAD_DIM), f32),
        compiler_params=params(8),
        cost_estimate=cost(2 * 2 * t * t * HEAD_DIM * 5 // 8, t * HEAD_DIM * 10),
        name="local_attn",
    )(q, k, v)


def column(row):
    return jnp.broadcast_to(row, (128, row.shape[1])).T


def attn_kernel(*refs):
    n = len(refs) - 6
    o_refs = refs[:n]
    q_ref, p_ref, y_ref, g_ref, attn_ref, stat_ref = refs[n:]
    t, c = q_ref.shape
    w = o_refs[0].shape[1]
    for i in range(t // ROWS):
        rows = chunk(i)
        squares = dots = 0.0
        for at in range(0, c, HEAD_DIM):
            cols = slice(at, at + HEAD_DIM)
            own = o_refs[at // w][rows, at % w : at % w + HEAD_DIM]
            attn = own + nn(q_ref[rows, cols], p_ref[at // HEAD_DIM])
            attn_ref[rows, cols] = attn
            squares = squares + attn * attn
            dots = dots + y_ref[rows, cols].astype(f32) * g_ref[:, cols] * attn
        stat_ref[0:1, rows] = jnp.sum(squares.T, axis=0, keepdims=True)
        stat_ref[1:2, rows] = jnp.sum(dots.T, axis=0, keepdims=True)


def attn_stats(locals_, q, prefix, y, gain):
    t, c = q.shape
    return pl.pallas_call(
        attn_kernel,
        in_specs=[VMEM] * (len(locals_) + 4),
        out_specs=(VMEM, VMEM),
        out_shape=(jax.ShapeDtypeStruct((t, c), f32), jax.ShapeDtypeStruct((2, t), f32)),
        compiler_params=params(8),
        cost_estimate=cost(2 * t * c * 128, t * c * 12),
        name="attn_stats",
    )(*locals_, q, prefix, y, gain)


def grad_kernel(attn_ref, y_ref, q_ref, s0, s1, s2, s3, g_ref, mixed_hbm, d_ref, term_ref, m_ref, sems):
    t, c = q_ref.shape
    stat = (s0[...] + s1[...]) + (s2[...] + s3[...])
    inv_row = lax.rsqrt(stat[0:1, :] / WIDTH + epsilon)
    scale_row = inv_row * inv_row * stat[1:2, :] / WIDTH
    total = [None] * (c // 256)
    copies = []
    for i in range(t // ROWS):
        rows = chunk(i)
        inv = column(inv_row[:, rows])
        scale = column(scale_row[:, rows])
        for at in range(0, c, HEAD_DIM):
            cols = slice(at, at + HEAD_DIM)
            attn = attn_ref[rows, cols]
            gain = g_ref[:, cols]
            m_ref[rows, cols] = (attn * inv * gain).astype(bf16)
            up = y_ref[rows, cols].astype(f32) * gain
            d_ref[rows, cols] = (inv * (up - attn * scale)).astype(bf16)
        copies.append(
            pltpu.make_async_copy(
                m_ref.at[pl.ds(i * ROWS, ROWS)], mixed_hbm.at[pl.ds(i * ROWS, ROWS)], sems.at[i]
            )
        )
        copies[-1].start()
        for p in range(c // 256):
            cols = slice(p * 256, p * 256 + 256)
            x = tn(q_ref[rows, cols], d_ref[rows, cols])
            total[p] = x if i == 0 else total[p] + x
    for p in range(c // 256):
        term_ref[2 * p] = total[p][:128, :128].astype(bf16)
        term_ref[2 * p + 1] = total[p][128:, 128:].astype(bf16)
    for copy in copies:
        copy.wait()


def grads_of_norm(attn, y, q, stats, gain):
    t, c = q.shape
    heads = c // HEAD_DIM
    return pl.pallas_call(
        grad_kernel,
        in_specs=[VMEM] * 8,
        out_specs=(ANY, VMEM, VMEM),
        out_shape=(
            jax.ShapeDtypeStruct((t, c), bf16),
            jax.ShapeDtypeStruct((t, c), bf16),
            jax.ShapeDtypeStruct((heads, 128, 128), bf16),
        ),
        scratch_shapes=[pltpu.VMEM((t, c), bf16), pltpu.SemaphoreType.DMA((t // ROWS,))],
        compiler_params=params(8),
        cost_estimate=cost(2 * t * c * 256, t * c * 12),
        name="grads_of_norm",
    )(attn, y, q, *stats, gain)


def back_kernel(head, q_ref, k_ref, v_ref, d_ref, p_ref, *refs):
    dq_hbm, dk_ref, dv_ref, dq_ref, sems = refs[-5:]
    t = q_ref.shape[0]
    cols = slice(head * HEAD_DIM, (head + 1) * HEAD_DIM)
    copies = []
    for i in range(t // ROWS):
        r, e = i * ROWS, (i + 1) * ROWS
        here = slice(r, e)
        q, k, v, d = q_ref[here, cols], k_ref[here, cols], v_ref[here, cols], d_ref[here, cols]
        dq = nt(d, p_ref[head]) + nn(masked(nt(d, v)), k)
        if r:
            dq = dq + nn(nt(d, v_ref[:r, cols]).astype(bf16), k_ref[:r, cols])
        dq_ref[here, :] = dq.astype(bf16)
        there = pl.ds(r, ROWS)
        copies.append(
            pltpu.make_async_copy(
                dq_ref.at[there], dq_hbm.at[there, pl.ds(head * HEAD_DIM, HEAD_DIM)], sems.at[i]
            )
        )
        copies[-1].start()
        dk = nn(masked(nt(v, d), True), q)
        dv = nn(masked(nt(k, q), True), d)
        if e < t:
            dk = dk + nn(nt(v, d_ref[e:, cols]).astype(bf16), q_ref[e:, cols])
            dv = dv + nn(nt(k, q_ref[e:, cols]).astype(bf16), d_ref[e:, cols])
        dk_ref[here, :] = dk
        dv_ref[here, :] = dv
    for copy in copies:
        copy.wait()


def local_back(q, k, v, d, prefix, dq, head):
    t, c = q.shape
    held = [] if dq is None else [dq]
    return pl.pallas_call(
        functools.partial(back_kernel, head),
        in_specs=[VMEM] * 5 + [ANY] * len(held),
        out_specs=(ANY, VMEM, VMEM),
        input_output_aliases={5: 0} if held else {},
        out_shape=(
            jax.ShapeDtypeStruct((t, c), bf16),
            jax.ShapeDtypeStruct((t, HEAD_DIM), f32),
            jax.ShapeDtypeStruct((t, HEAD_DIM), f32),
        ),
        scratch_shapes=[
            pltpu.VMEM((t, HEAD_DIM), bf16),
            pltpu.SemaphoreType.DMA((t // ROWS,)),
        ],
        compiler_params=params(8),
        cost_estimate=cost(6 * 2 * t * t * HEAD_DIM * 5 // 8, t * HEAD_DIM * 18),
        name="local_back",
    )(q, k, v, d, prefix, *held)


def final_kernel(*refs):
    n = (len(refs) - 8) // 2
    dk_refs, dv_refs = refs[:n], refs[n : 2 * n]
    k_ref, v_ref, s_ref, ok_hbm, ov_hbm, ok_ref, ov_ref, sems = refs[2 * n :]
    t, c = k_ref.shape
    w = dk_refs[0].shape[1]
    copies = []
    for i in range(t // ROWS):
        rows = chunk(i)
        for at in range(0, c, HEAD_DIM):
            cols = slice(at, at + HEAD_DIM)
            h = at // HEAD_DIM
            part = slice(at % w, at % w + HEAD_DIM)
            ok_ref[rows, cols] = (dk_refs[at // w][rows, part] + nt(v_ref[rows, cols], s_ref[h])).astype(bf16)
            ov_ref[rows, cols] = (dv_refs[at // w][rows, part] + nn(k_ref[rows, cols], s_ref[h])).astype(bf16)
        for ref, hbm in ((ok_ref, ok_hbm), (ov_ref, ov_hbm)):
            there = pl.ds(i * ROWS, ROWS)
            copies.append(pltpu.make_async_copy(ref.at[there], hbm.at[there], sems.at[len(copies)]))
            copies[-1].start()
    for copy in copies:
        copy.wait()


def finish(dks, dvs, k, v, suffix):
    t, c = k.shape
    return pl.pallas_call(
        final_kernel,
        in_specs=[VMEM] * (2 * len(dks) + 3),
        out_specs=(ANY, ANY),
        out_shape=(jax.ShapeDtypeStruct((t, c), bf16),) * 2,
        scratch_shapes=[
            pltpu.VMEM((t, c), bf16),
            pltpu.VMEM((t, c), bf16),
            pltpu.SemaphoreType.DMA((2 * t // ROWS,)),
        ],
        compiler_params=params(8),
        cost_estimate=cost(4 * t * c * 128, t * c * 16),
        name="finish",
    )(*dks, *dvs, k, v, suffix)


NZ, NX = 8, 4


def step_pairs(reverse, dz=0, dx=0, swap=False):
    pairs = []
    for i in range(NZ * NX * 2):
        z, x, c = i // 8, (i // 2) % 4, i % 2
        j = ((z + dz) % NZ * NX + (x + dx) % NX) * 2 + (1 - c if swap else c)
        pairs.append((63 - i, 63 - j) if reverse else (i, j))
    return pairs


def places(reverse):
    index = lax.axis_index("seq")
    index = 63 - index if reverse else index
    z, x, c = index >> 3, (index >> 1) & 3, index & 1
    low, high = (z + 7) & 7, (z + 1) & 7
    up, down = (z + 3) & 7, (z + 5) & 7
    return (
        c == 0,
        tuple(x >= k for k in (1, 2, 3)),
        z >= 1,
        z == 7,
        (low < up, z < up, high < up),
        (low < down, z < down),
    )


def exclusive_sum(own, reverse, masks):
    def send(a, **step):
        return lax.ppermute(a, "seq", step_pairs(reverse, **step))

    first, west, south, north, up, down = masks
    n = own.shape[0] // 2
    mine = jnp.where(first, own[:n], own[n:])
    other = jnp.where(first, own[n:], own[:n])
    got = send(other, swap=True)
    chip = (mine.astype(f32) + got.astype(f32)).astype(bf16)
    row = chip.astype(f32)
    before = jnp.zeros_like(row)
    for k in (1, 3, 2):
        r = send(chip, dx=k).astype(f32)
        row = row + r
        before = before + jnp.where(west[k - 1], r, 0.0)
    plane = row.astype(bf16)
    below = send(plane, dz=1).astype(f32)
    above = send(plane, dz=-1).astype(f32)
    near = jnp.where(south, below, 0.0) + jnp.where(north, above, 0.0)

    def lacking(flags):
        return sum(jnp.where(m, p, 0.0) for m, p in zip(flags, (below, row, above))).astype(bf16)

    far = send(lacking(up), dz=3).astype(f32)
    far = far + send(lacking(down), dz=-3).astype(f32)
    e0 = before + near + far
    e1 = e0 + jnp.where(first, mine, got).astype(f32)
    e0, e1 = e0.astype(bf16), e1.astype(bf16)
    keep = jnp.where(first, e0, e1)
    back = send(jnp.where(first, e1, e0), swap=True)
    return jnp.where(first, jnp.concatenate([keep, back]), jnp.concatenate([back, keep]))


def head_parts(a):
    return [a] + [
        lax.ppermute(a, "head", [(i, (i + k) % 4) for i in range(4)]) for k in (1, 3, 2)
    ]


PARTS = 4


def shards(q, k, v, y, gain):
    gain = gain[None, :]
    first, last = places(False), places(True)
    first, last, k, v = lax.optimization_barrier((first, last, k, v))
    in_hbm = [pltpu.with_memory_space_constraint(a, pltpu.HBM) for a in (k, v)]
    prefix = exclusive_sum(block_state(*in_hbm), False, first)
    locals_ = []
    for i in range(PARTS):
        locals_.append(local_attn(q, k, v, i))
    attn, stats = attn_stats(locals_, q, prefix, y, gain)
    mixed, d, term = grads_of_norm(attn, y, q, head_parts(stats), gain)
    suffix = exclusive_sum(term, True, last)
    dq, dks, dvs = None, [], []
    for i in range(PARTS):
        dq, dk, dv = local_back(q, k, v, d, prefix, dq, i)
        dks.append(dk)
        dvs.append(dv)
    dk, dv = finish(dks, dvs, k, v, suffix)
    return mixed, dq, dk, dv


def solution(mesh):
    wide = P("seq", "head")
    return jax.shard_map(
        shards,
        mesh=mesh,
        in_specs=(wide, wide, wide, wide, P("head")),
        out_specs=(wide, wide, wide, wide),
        check_vma=False,
    )
```

```python
import functools

import jax
import jax.numpy as jnp
from jax import lax
from jax.experimental import pallas as pl
from jax.experimental.pallas import tpu as pltpu
from jax.sharding import PartitionSpec as P


HEAD_DIM = 128
WIDTH = 2048
epsilon = 1e-06
ROWS = 256

f32 = jnp.float32
bf16 = jnp.bfloat16


def nn(a, b):
    return lax.dot_general(a, b, (((1,), (0,)), ((), ())), preferred_element_type=f32)


def nt(a, b):
    return lax.dot_general(a, b, (((1,), (1,)), ((), ())), preferred_element_type=f32)


def tn(a, b):
    return lax.dot_general(a, b, (((0,), (0,)), ((), ())), preferred_element_type=f32)


def params(mib=24):
    return pltpu.CompilerParams(vmem_limit_bytes=mib << 20)


def cost(flops, nbytes):
    return pl.CostEstimate(flops=flops, bytes_accessed=nbytes, transcendentals=0)


VMEM = pl.BlockSpec(memory_space=pltpu.VMEM)
ANY = pl.BlockSpec(memory_space=pl.ANY)


def chunk(i):
    return slice(i * ROWS, (i + 1) * ROWS)


def outer_kernel(a_hbm, b_hbm, s_ref, a_ref, b_ref, sems):
    t, c = a_ref.shape
    n = t // ROWS
    copies = []
    for i in range(n):
        for hbm, ref in ((a_hbm, a_ref), (b_hbm, b_ref)):
            rows = pl.ds(i * ROWS, ROWS)
            copy = pltpu.make_async_copy(hbm.at[rows], ref.at[rows], sems.at[len(copies)])
            copy.start()
            copies.append(copy)
    total = [None] * (c // 256)
    for i in range(n):
        copies[2 * i].wait()
        copies[2 * i + 1].wait()
        for p in range(c // 256):
            cols = slice(p * 256, p * 256 + 256)
            x = tn(a_ref[chunk(i), cols], b_ref[chunk(i), cols])
            total[p] = x if i == 0 else total[p] + x
    for p in range(c // 256):
        s_ref[2 * p] = total[p][:128, :128].astype(bf16)
        s_ref[2 * p + 1] = total[p][128:, 128:].astype(bf16)


def block_state(a, b):
    t, c = a.shape
    heads = c // HEAD_DIM
    return pl.pallas_call(
        outer_kernel,
        in_specs=[ANY, ANY],
        out_specs=VMEM,
        out_shape=jax.ShapeDtypeStruct((heads, 128, 128), bf16),
        scratch_shapes=[
            pltpu.VMEM((t, c), bf16),
            pltpu.VMEM((t, c), bf16),
            pltpu.SemaphoreType.DMA((2 * t // ROWS,)),
        ],
        compiler_params=params(8),
        cost_estimate=cost(2 * t * c * 256, 2 * t * c * 2),
        name="block_state",
    )(a, b)


def masked(x, upper=False):
    row = lax.broadcasted_iota(jnp.int32, x.shape, 0)
    col = lax.broadcasted_iota(jnp.int32, x.shape, 1)
    return jnp.where((row <= col) if upper else (row >= col), x, 0.0).astype(bf16)


def local_kernel(head, q_ref, k_ref, v_ref, o_ref):
    t = q_ref.shape[0]
    cols = slice(head * HEAD_DIM, (head + 1) * HEAD_DIM)
    for r in range(0, t, ROWS):
        q = q_ref[r : r + ROWS, cols]
        w = masked(nt(q, k_ref[r : r + ROWS, cols]))
        o = nn(w, v_ref[r : r + ROWS, cols])
        if r:
            w = nt(q, k_ref[:r, cols]).astype(bf16)
            o = o + nn(w, v_ref[:r, cols])
        o_ref[r : r + ROWS, :] = o


def local_attn(q, k, v, head):
    t = q.shape[0]
    return pl.pallas_call(
        functools.partial(local_kernel, head),
        in_specs=[VMEM] * 3,
        out_specs=VMEM,
        out_shape=jax.ShapeDtypeStruct((t, HEAD_DIM), f32),
        compiler_params=params(8),
        cost_estimate=cost(2 * 2 * t * t * HEAD_DIM * 5 // 8, t * HEAD_DIM * 10),
        name="local_attn",
    )(q, k, v)


def turned_kernel(head, q_ref, k_ref, w_ref):
    t = q_ref.shape[0]
    cols = slice(head * HEAD_DIM, (head + 1) * HEAD_DIM)
    for r in range(0, t, ROWS):
        e = r + ROWS
        k = k_ref[r:e, cols]
        w_ref[r:e, r:e] = masked(nt(k, q_ref[r:e, cols]), True)
        if e < t:
            w_ref[r:e, e:] = nt(k, q_ref[e:, cols]).astype(bf16)


def turned_weights(q, k, head):
    t = q.shape[0]
    return pl.pallas_call(
        functools.partial(turned_kernel, head),
        in_specs=[VMEM] * 2,
        out_specs=VMEM,
        out_shape=jax.ShapeDtypeStruct((t, t), bf16),
        compiler_params=params(8),
        cost_estimate=cost(2 * t * t * HEAD_DIM * 5 // 8, t * t),
        name="turned_weights",
    )(q, k)


def column(row):
    return jnp.broadcast_to(row, (128, row.shape[1])).T


def attn_kernel(*refs):
    n = len(refs) - 6
    o_refs = refs[:n]
    q_ref, p_ref, y_ref, g_ref, attn_ref, stat_ref = refs[n:]
    t, c = q_ref.shape
    w = o_refs[0].shape[1]
    for i in range(t // ROWS):
        rows = chunk(i)
        squares = dots = 0.0
        for at in range(0, c, HEAD_DIM):
            cols = slice(at, at + HEAD_DIM)
            own = o_refs[at // w][rows, at % w : at % w + HEAD_DIM]
            attn = own + nn(q_ref[rows, cols], p_ref[at // HEAD_DIM])
            attn_ref[rows, cols] = attn
            squares = squares + attn * attn
            dots = dots + y_ref[rows, cols].astype(f32) * g_ref[:, cols] * attn
        stat_ref[0:1, rows] = jnp.sum(squares.T, axis=0, keepdims=True)
        stat_ref[1:2, rows] = jnp.sum(dots.T, axis=0, keepdims=True)


def attn_stats(locals_, q, prefix, y, gain):
    t, c = q.shape
    return pl.pallas_call(
        attn_kernel,
        in_specs=[VMEM] * (len(locals_) + 4),
        out_specs=(VMEM, VMEM),
        out_shape=(jax.ShapeDtypeStruct((t, c), f32), jax.ShapeDtypeStruct((2, t), f32)),
        compiler_params=params(8),
        cost_estimate=cost(2 * t * c * 128, t * c * 12),
        name="attn_stats",
    )(*locals_, q, prefix, y, gain)


def grad_kernel(attn_ref, y_ref, q_ref, s0, s1, s2, s3, g_ref, mixed_hbm, d_ref, term_ref, m_ref, sems):
    t, c = q_ref.shape
    stat = (s0[...] + s1[...]) + (s2[...] + s3[...])
    inv_row = lax.rsqrt(stat[0:1, :] / WIDTH + epsilon)
    scale_row = inv_row * inv_row * stat[1:2, :] / WIDTH
    total = [None] * (c // 256)
    copies = []
    for i in range(t // ROWS):
        rows = chunk(i)
        inv = column(inv_row[:, rows])
        scale = column(scale_row[:, rows])
        for at in range(0, c, HEAD_DIM):
            cols = slice(at, at + HEAD_DIM)
            attn = attn_ref[rows, cols]
            gain = g_ref[:, cols]
            m_ref[rows, cols] = (attn * inv * gain).astype(bf16)
            up = y_ref[rows, cols].astype(f32) * gain
            d_ref[rows, cols] = (inv * (up - attn * scale)).astype(bf16)
        copies.append(
            pltpu.make_async_copy(
                m_ref.at[pl.ds(i * ROWS, ROWS)], mixed_hbm.at[pl.ds(i * ROWS, ROWS)], sems.at[i]
            )
        )
        copies[-1].start()
        for p in range(c // 256):
            cols = slice(p * 256, p * 256 + 256)
            x = tn(q_ref[rows, cols], d_ref[rows, cols])
            total[p] = x if i == 0 else total[p] + x
    for p in range(c // 256):
        term_ref[2 * p] = total[p][:128, :128].astype(bf16)
        term_ref[2 * p + 1] = total[p][128:, 128:].astype(bf16)
    for copy in copies:
        copy.wait()


def grads_of_norm(attn, y, q, stats, gain):
    t, c = q.shape
    heads = c // HEAD_DIM
    return pl.pallas_call(
        grad_kernel,
        in_specs=[VMEM] * 8,
        out_specs=(ANY, VMEM, VMEM),
        out_shape=(
            jax.ShapeDtypeStruct((t, c), bf16),
            jax.ShapeDtypeStruct((t, c), bf16),
            jax.ShapeDtypeStruct((heads, 128, 128), bf16),
        ),
        scratch_shapes=[pltpu.VMEM((t, c), bf16), pltpu.SemaphoreType.DMA((t // ROWS,))],
        compiler_params=params(8),
        cost_estimate=cost(2 * t * c * 256, t * c * 12),
        name="grads_of_norm",
    )(attn, y, q, *stats, gain)


def query_kernel(head, k_ref, v_ref, d_ref, p_ref, dq_ref):
    t = k_ref.shape[0]
    cols = slice(head * HEAD_DIM, (head + 1) * HEAD_DIM)
    for r in range(0, t, ROWS):
        here = slice(r, r + ROWS)
        d = d_ref[here, cols]
        dq = nt(d, p_ref[head]) + nn(masked(nt(d, v_ref[here, cols])), k_ref[here, cols])
        if r:
            dq = dq + nn(nt(d, v_ref[:r, cols]).astype(bf16), k_ref[:r, cols])
        dq_ref[here, :] = dq.astype(bf16)


def grad_query(k, v, d, prefix, head):
    t = k.shape[0]
    return pl.pallas_call(
        functools.partial(query_kernel, head),
        in_specs=[VMEM] * 4,
        out_specs=VMEM,
        out_shape=jax.ShapeDtypeStruct((t, HEAD_DIM), bf16),
        compiler_params=params(8),
        cost_estimate=cost(2 * 2 * t * t * HEAD_DIM * 5 // 8, t * HEAD_DIM * 10),
        name="grad_query",
    )(k, v, d, prefix)


def back_kernel(head, q_ref, v_ref, d_ref, w_ref, dk_ref, dv_ref):
    t = q_ref.shape[0]
    cols = slice(head * HEAD_DIM, (head + 1) * HEAD_DIM)
    for r in range(0, t, ROWS):
        e = r + ROWS
        here = slice(r, e)
        v = v_ref[here, cols]
        dk = nn(masked(nt(v, d_ref[here, cols]), True), q_ref[here, cols])
        if e < t:
            dk = dk + nn(nt(v, d_ref[e:, cols]).astype(bf16), q_ref[e:, cols])
        dk_ref[here, :] = dk
        dv_ref[here, :] = nn(w_ref[here, r:], d_ref[r:, cols])


def local_back(q, v, d, turned, head):
    t = q.shape[0]
    return pl.pallas_call(
        functools.partial(back_kernel, head),
        in_specs=[VMEM] * 4,
        out_specs=(VMEM, VMEM),
        out_shape=(jax.ShapeDtypeStruct((t, HEAD_DIM), f32),) * 2,
        compiler_params=params(8),
        cost_estimate=cost(3 * 2 * t * t * HEAD_DIM * 5 // 8, t * HEAD_DIM * 14),
        name="local_back",
    )(q, v, d, turned)


def write_kernel(*refs):
    n = len(refs) - 2
    parts, out, sems = refs[:n], refs[n], refs[n + 1]
    copies = [
        pltpu.make_async_copy(part, out.at[:, pl.ds(i * HEAD_DIM, HEAD_DIM)], sems.at[i])
        for i, part in enumerate(parts)
    ]
    for copy in copies:
        copy.start()
    for copy in copies:
        copy.wait()


def side_by_side(parts):
    t = parts[0].shape[0]
    n = len(parts)
    return pl.pallas_call(
        write_kernel,
        in_specs=[VMEM] * n,
        out_specs=ANY,
        out_shape=jax.ShapeDtypeStruct((t, n * HEAD_DIM), bf16),
        scratch_shapes=[pltpu.SemaphoreType.DMA((n,))],
        compiler_params=params(8),
        cost_estimate=cost(0, 4 * t * n * HEAD_DIM),
        name="side_by_side",
    )(*parts)


def final_kernel(*refs):
    n = (len(refs) - 8) // 2
    dk_refs, dv_refs = refs[:n], refs[n : 2 * n]
    k_ref, v_ref, s_ref, ok_hbm, ov_hbm, ok_ref, ov_ref, sems = refs[2 * n :]
    t, c = k_ref.shape
    w = dk_refs[0].shape[1]
    copies = []
    for i in range(t // ROWS):
        rows = chunk(i)
        for at in range(0, c, HEAD_DIM):
            cols = slice(at, at + HEAD_DIM)
            h = at // HEAD_DIM
            part = slice(at % w, at % w + HEAD_DIM)
            ok_ref[rows, cols] = (dk_refs[at // w][rows, part] + nt(v_ref[rows, cols], s_ref[h])).astype(bf16)
            ov_ref[rows, cols] = (dv_refs[at // w][rows, part] + nn(k_ref[rows, cols], s_ref[h])).astype(bf16)
        for ref, hbm in ((ok_ref, ok_hbm), (ov_ref, ov_hbm)):
            there = pl.ds(i * ROWS, ROWS)
            copies.append(pltpu.make_async_copy(ref.at[there], hbm.at[there], sems.at[len(copies)]))
            copies[-1].start()
    for copy in copies:
        copy.wait()


def finish(dks, dvs, k, v, suffix):
    t, c = k.shape
    return pl.pallas_call(
        final_kernel,
        in_specs=[VMEM] * (2 * len(dks) + 3),
        out_specs=(ANY, ANY),
        out_shape=(jax.ShapeDtypeStruct((t, c), bf16),) * 2,
        scratch_shapes=[
            pltpu.VMEM((t, c), bf16),
            pltpu.VMEM((t, c), bf16),
            pltpu.SemaphoreType.DMA((2 * t // ROWS,)),
        ],
        compiler_params=params(8),
        cost_estimate=cost(4 * t * c * 128, t * c * 16),
        name="finish",
    )(*dks, *dvs, k, v, suffix)


NZ, NX = 8, 4


def step_pairs(reverse, dz=0, dx=0, swap=False):
    pairs = []
    for i in range(NZ * NX * 2):
        z, x, c = i // 8, (i // 2) % 4, i % 2
        j = ((z + dz) % NZ * NX + (x + dx) % NX) * 2 + (1 - c if swap else c)
        pairs.append((63 - i, 63 - j) if reverse else (i, j))
    return pairs


def places(reverse):
    index = lax.axis_index("seq")
    index = 63 - index if reverse else index
    z, x, c = index >> 3, (index >> 1) & 3, index & 1
    low, high = (z + 7) & 7, (z + 1) & 7
    up, down = (z + 3) & 7, (z + 5) & 7
    return (
        c == 0,
        tuple(x >= k for k in (1, 2, 3)),
        z >= 1,
        z == 7,
        (low < up, z < up, high < up),
        (low < down, z < down),
    )


def exclusive_sum(own, reverse, masks):
    def send(a, **step):
        return lax.ppermute(a, "seq", step_pairs(reverse, **step))

    first, west, south, north, up, down = masks
    n = own.shape[0] // 2
    mine = jnp.where(first, own[:n], own[n:])
    other = jnp.where(first, own[n:], own[:n])
    got = send(other, swap=True)
    chip = (mine.astype(f32) + got.astype(f32)).astype(bf16)
    row = chip.astype(f32)
    before = jnp.zeros_like(row)
    for k in (1, 3, 2):
        r = send(chip, dx=k).astype(f32)
        row = row + r
        before = before + jnp.where(west[k - 1], r, 0.0)
    plane = row.astype(bf16)
    below = send(plane, dz=1).astype(f32)
    above = send(plane, dz=-1).astype(f32)
    near = jnp.where(south, below, 0.0) + jnp.where(north, above, 0.0)

    def lacking(flags):
        return sum(jnp.where(m, p, 0.0) for m, p in zip(flags, (below, row, above))).astype(bf16)

    far = send(lacking(up), dz=3).astype(f32)
    far = far + send(lacking(down), dz=-3).astype(f32)
    e0 = before + near + far
    e1 = e0 + jnp.where(first, mine, got).astype(f32)
    e0, e1 = e0.astype(bf16), e1.astype(bf16)
    keep = jnp.where(first, e0, e1)
    back = send(jnp.where(first, e1, e0), swap=True)
    return jnp.where(first, jnp.concatenate([keep, back]), jnp.concatenate([back, keep]))


def head_parts(a):
    return [a] + [
        lax.ppermute(a, "head", [(i, (i + k) % 4) for i in range(4)]) for k in (1, 3, 2)
    ]


PARTS = 4


def shards(q, k, v, y, gain):
    gain = gain[None, :]
    first, last = places(False), places(True)
    first, last, k, v = lax.optimization_barrier((first, last, k, v))
    in_hbm = [pltpu.with_memory_space_constraint(a, pltpu.HBM) for a in (k, v)]
    prefix = exclusive_sum(block_state(*in_hbm), False, first)
    locals_, turned = [], []
    for i in range(PARTS):
        locals_.append(local_attn(q, k, v, i))
        turned.append(turned_weights(q, k, i))
    attn, stats = attn_stats(locals_, q, prefix, y, gain)
    mixed, d, term = grads_of_norm(attn, y, q, head_parts(stats), gain)
    suffix = exclusive_sum(term, True, last)
    dqs, dks, dvs = [], [], []
    for i in range(PARTS):
        dqs.append(grad_query(k, v, d, prefix, i))
        dk, dv = local_back(q, v, d, turned[i], i)
        dks.append(dk)
        dvs.append(dv)
    dq = side_by_side(dqs)
    dk, dv = finish(dks, dvs, k, v, suffix)
    return mixed, dq, dk, dv


def solution(mesh):
    wide = P("seq", "head")
    return jax.shard_map(
        shards,
        mesh=mesh,
        in_specs=(wide, wide, wide, wide, P("head")),
        out_specs=(wide, wide, wide, wide),
        check_vma=False,
    )
```
